32 devices in a mesh: site: 4 (over y, x), sector: 8 (over z, core).
Axes of the slice: x: 2, y: 2, z: 4, core: 2. Of those that a mesh axis runs over, the one named last changes fastest.
Arguments:
- boundary: bfloat16 [4, 2048, 32, 256], P('site', 'sector'), may hold values from -0.375 to 0.375
- peps_row: bfloat16 [4, 32, 8], P('site'), may hold values from -1 to 1
- sketch: bfloat16 [4, 2048, 8, 256], P('site', 'sector'), may hold values from -0.125 to 0.125
- charges: int32 [4, 8], P('site'), may hold values from -1 to 1
- left_edge: bfloat16 [512, 2048], P(None, 'sector'), may hold values from -6 to 6
Outputs:
- environments: float32 [4, 512, 2048], P('site', None, 'sector')
The draws below stay inside these ranges and needn't reach their ends.
Inputs may be any that keep to these rules, and one draw needn't show every extreme that they name: `charges`: each entry is a charge change of -1, 0 or +1.
All inputs are finite; a program needn't handle non-finite values.
Results may differ from the reference program's by a relative error of at most 0.0003.
Values sent between devices are 32-bit elements; how exact they have to be, the bound alone decides.
A program may use at most 64 MiB of HBM per device.

```python
import jax
import jax.numpy as jnp
from jax import lax

W = 256
P_SIZE = 32
D = 8
ROWS = 512
SITES = 4
CHI = 2048
N_SECTOR = 8


def place_ends(values, own_key, least, high):
    shape = values.shape
    spot = [jax.random.randint(jax.random.fold_in(own_key, axis), (), 0, shape[axis]) for axis in range(len(shape))]
    values = values.at[tuple(spot)].set(least)
    longest = shape.index(max(shape))
    spot[longest] = (spot[longest] + 1) % shape[longest]
    return values.at[tuple(spot)].set(high)


def level_of(stream_key, extent, pieces, low, top_value):
    level, own = 1.0, jax.random.fold_in(stream_key, 6)
    for axis_at, blocks in pieces:
        heights = jnp.exp(jax.random.uniform(jax.random.fold_in(own, axis_at), (blocks,), jnp.float32, low / len(pieces), top_value / len(pieces)))
        level = level * jnp.repeat(heights, extent[axis_at] // blocks).reshape([-1 if axis == axis_at else 1 for axis in range(len(extent))])
    return level


def centred(own_key, extent, scale, bound, split=(), held_as=jnp.bfloat16):
    level = level_of(own_key, extent, split, -0.22, 0.18) if split else 1.0
    entries = jax.random.normal(own_key, extent, jnp.float32) * scale * level
    return jnp.minimum(jnp.maximum(entries, -bound), bound).astype(held_as)


def setup_inputs(seed: int = 0) -> dict:
    key_of = jax.random.split(jax.random.key(seed), 6)
    return {
        "boundary": centred(key_of[0], (SITES, CHI, P_SIZE, W), W ** -0.5, 0.375, ((0, 4), (1, 8))),
        "peps_row": centred(key_of[1], (SITES, P_SIZE, D), P_SIZE ** -0.5, 1.0, ((0, 4),)),
        "sketch": centred(key_of[2], (SITES, CHI, D, W), (W * D) ** -0.5, 0.125, ((0, 4), (1, 8))),
        "charges": place_ends(jax.random.randint(key_of[3], (SITES, D), -1, 2), jax.random.fold_in(key_of[3], 1), -1, 1).astype(jnp.int32),
        "left_edge": centred(key_of[4], (ROWS, CHI), 1.0, 6.0, ((1, 8),)),
    }


def reference(boundary, peps_row, sketch, charges, left_edge):
    absorbed = jnp.einsum('jipv,jpl->jilv', boundary.astype(jnp.float32), peps_row.astype(jnp.float32), precision=lax.Precision.HIGHEST)

    def absorb_site(state_rows, inputs):
        block_tensor, block_sketch, charge_row = inputs
        block_tensor = block_tensor.reshape(N_SECTOR, W, D, W)
        block_sketch = block_sketch.astype(jnp.float32).reshape(N_SECTOR, W, D, W)
        onehot = (charge_row[:, None] == jnp.arange(-1, 2, dtype=jnp.int32)[None, :]).astype(jnp.float32)
        transfer = jnp.einsum('bwlv,bvlu,ls->bswu', block_tensor, block_sketch, onehot, precision=lax.Precision.HIGHEST)
        blocked = state_rows.reshape(ROWS, N_SECTOR, W)
        parts = jnp.einsum('rbw,bswu->srbu', blocked, transfer, precision=lax.Precision.HIGHEST)
        empty_rows = jnp.zeros((ROWS, 1, W), jnp.float32)
        updated = parts[1] + jnp.concatenate([empty_rows, parts[2][:, :-1]], axis=1) + jnp.concatenate([parts[0][:, 1:], empty_rows], axis=1)
        updated = updated.reshape(ROWS, N_SECTOR * W)
        return updated, updated

    start_rows = left_edge.astype(jnp.float32)
    final_rows, environments = lax.scan(absorb_site, start_rows, (absorbed, sketch, charges))
    return environments
```

```python
import functools

import jax
import jax.numpy as jnp
from jax import lax
from jax.experimental import pallas as pl
from jax.experimental.pallas import tpu as pltpu
from jax.sharding import PartitionSpec as P

MESH = pl.DeviceIdType.MESH
CHUNK_ROWS = 32
LAG = 3
LAG_FIRST = 4
SLABS = 4
DOT_ROWS = 128


def dot(a, b):
    return jnp.dot(a, b, preferred_element_type=jnp.float32)


def split(x):
    high = x.astype(jnp.bfloat16)
    low = (x - high.astype(jnp.float32)).astype(jnp.bfloat16)
    return high, low


def iota(shape, axis):
    return lax.broadcasted_iota(jnp.int32, shape, axis)


def kernel(
    sites,
    sectors,
    width,
    phys,
    depth,
    boundary_ref,
    peps_ref,
    sketch_ref,
    charges_ref,
    left_ref,
    total,
    boundary,
    sketch,
    peps,
    charges,
    left,
    absorbed,
    sorted_sketch,
    map_high,
    map_low,
    state,
    from_below,
    from_above,
    upward,
    downward,
    boundary_sem,
    small_sem,
    state_send,
    state_recv,
    up_send,
    up_recv,
    down_send,
    down_recv,
):
    site = lax.axis_index("site")
    sector = lax.axis_index("sector")
    rows = left_ref.shape[0]
    chunks = rows // CHUNK_ROWS
    f32, bf16 = jnp.float32, jnp.bfloat16

    peps_copy = pltpu.make_async_copy(peps_ref, peps, small_sem.at[0])
    charges_copy = pltpu.make_async_copy(charges_ref, charges, small_sem.at[1])
    sketch_copy = pltpu.make_async_copy(sketch_ref, sketch, small_sem.at[2])
    left_copy = pltpu.make_async_copy(left_ref, left, small_sem.at[3])
    peps_copy.start()
    charges_copy.start()
    sketch_copy.start()
    slab_rows = width // SLABS
    slabs = []
    for i in range(SLABS):
        part = pl.ds(i * slab_rows * phys, slab_rows * phys)
        copy = pltpu.make_async_copy(boundary_ref.at[part], boundary.at[part], boundary_sem.at[i])
        copy.start()
        slabs.append(copy)

    @pl.when(site == 0)
    def _():
        left_copy.start()

    barrier = pltpu.get_barrier_semaphore()
    has_prev, has_next = site > 0, site < sites - 1
    has_below, has_above = sector > 0, sector < sectors - 1

    def greet(condition, target):
        @pl.when(condition)
        def _():
            pl.semaphore_signal(barrier, inc=1, device_id=target, device_id_type=MESH)

    prev_id, next_id = (site - 1, sector), (site + 1, sector)
    below_id, above_id = (site, sector - 1), (site, sector + 1)
    greet(has_prev, prev_id)
    greet(has_next, next_id)
    greet(has_below, below_id)
    greet(has_above, above_id)

    @pl.when(jnp.logical_not(has_below))
    def _():
        from_below[...] = jnp.zeros_like(from_below)

    @pl.when(jnp.logical_not(has_above))
    def _():
        from_above[...] = jnp.zeros_like(from_above)

    group = width // phys
    size = group * depth
    run = width // depth
    order = (
        iota((width, width), 1) == (iota((width, width), 0) % run) * depth + iota((width, width), 0) // run
    ).astype(f32).astype(bf16)
    pick = (iota((size, depth), 0) // group == iota((size, depth), 1)).astype(f32).astype(bf16)
    tile = (iota((phys, width), 1) % phys == iota((phys, width), 0)).astype(f32).astype(bf16)
    same = iota((size, width), 0) % group == iota((size, width), 1) // phys
    peps_copy.wait()
    charges_copy.wait()
    by_row = dot(pick, peps[...]).astype(bf16)
    spread = jnp.where(same, dot(by_row, tile), 0.0).astype(bf16)
    flags = [
        [(charges[0, l] == s - 1).astype(f32) for l in range(depth)] for s in range(3)
    ]

    sketch_copy.wait()
    for g in range(depth):
        moved = dot(order, sketch[pl.ds(g * width, width), :]).astype(bf16)
        for l in range(depth):
            sorted_sketch[l, pl.ds(g * run, run), :] = moved[l * run : (l + 1) * run]

    def absorb(g):
        grown = dot(spread, boundary[pl.ds(g * group * phys, width), :])
        for l in range(depth):
            absorbed[l, pl.ds(g * group, group), :] = grown[l * group : (l + 1) * group]

    def build(i):
        part = pl.ds(i * DOT_ROWS, DOT_ROWS)
        sums = [None] * 3
        for l in range(depth):
            high, low = split(absorbed[l, part])
            both = dot(jnp.concatenate([high, low], axis=0), sorted_sketch[l])
            product = both[:DOT_ROWS] + both[DOT_ROWS:]
            for s in range(3):
                term = flags[s][l] * product
                sums[s] = term if sums[s] is None else sums[s] + term
        for s in range(3):
            high, low = split(sums[s])
            map_high[part, pl.ds(s * width, width)] = high
            map_low[part, pl.ds(s * width, width)] = low

    for i in range(SLABS):
        slabs[i].wait()
        for g in range(i * slab_rows // group, (i + 1) * slab_rows // group):
            absorb(g)
        for b in range(width // DOT_ROWS):
            if i * slab_rows < (b + 1) * DOT_ROWS <= (i + 1) * slab_rows:
                build(b)

    @pl.when(site == 0)
    def _():
        left_copy.wait()
        state[...] = left[...].astype(f32)

    degree = (
        has_prev.astype(jnp.int32)
        + has_next.astype(jnp.int32)
        + has_below.astype(jnp.int32)
        + has_above.astype(jnp.int32)
    )
    pl.semaphore_wait(barrier, degree)

    def at(ref, k):
        return ref.at[pl.ds(k * CHUNK_ROWS, CHUNK_ROWS)]

    def state_copy(k):
        return pltpu.make_async_remote_copy(
            src_ref=at(total, k), dst_ref=at(state, k), send_sem=state_send.at[k],
            recv_sem=state_recv.at[k], device_id=next_id, device_id_type=MESH,
        )

    def up_copy(k):
        return pltpu.make_async_remote_copy(
            src_ref=at(upward, k), dst_ref=at(from_below, k), send_sem=up_send.at[k],
            recv_sem=up_recv.at[k], device_id=above_id, device_id_type=MESH,
        )

    def down_copy(k):
        return pltpu.make_async_remote_copy(
            src_ref=at(downward, k), dst_ref=at(from_above, k), send_sem=down_send.at[k],
            recv_sem=down_recv.at[k], device_id=below_id, device_id_type=MESH,
        )

    def advance(k):
        @pl.when(has_prev)
        def _():
            state_copy(k).wait_recv()

        high, low = split(at(state, k)[...])
        both = jnp.concatenate([high, low], axis=0)

        def part(s):
            columns = pl.ds(s * width, width)
            twice = dot(both, map_high[:, columns])
            return twice[:CHUNK_ROWS] + (twice[CHUNK_ROWS:] + dot(high, map_low[:, columns]))

        at(upward, k)[...] = part(2)
        at(downward, k)[...] = part(0)
        at(total, k)[...] = part(1)

        @pl.when(has_above)
        def _():
            up_copy(k).start()

        @pl.when(has_below)
        def _():
            down_copy(k).start()

    def finish(k):
        @pl.when(has_below)
        def _():
            up_copy(k).wait_recv()

        @pl.when(has_above)
        def _():
            down_copy(k).wait_recv()

        at(total, k)[...] += at(from_below, k)[...] + at(from_above, k)[...]

        @pl.when(has_next)
        def _():
            state_copy(k).start()

    def stream(lag):
        for k in range(chunks + lag):
            if k < chunks:
                advance(k)
            if k >= lag:
                finish(k - lag)

    @pl.when(site == 0)
    def _():
        stream(LAG_FIRST)

    @pl.when(site > 0)
    def _():
        stream(LAG)

    for k in range(chunks):
        @pl.when(has_above)
        def _():
            up_copy(k).wait_send()

        @pl.when(has_below)
        def _():
            down_copy(k).wait_send()

        @pl.when(has_next)
        def _():
            state_copy(k).wait_send()


def store(total, out_ref, sem):
    copy = pltpu.make_async_copy(total, out_ref, sem)
    copy.start()
    copy.wait()


def local(sites, sectors, boundary, peps_row, sketch, charges, left_edge):
    _, width, phys, inner = boundary.shape
    depth = peps_row.shape[2]
    rows = left_edge.shape[0]
    chunks = rows // CHUNK_ROWS
    f32, bf16 = jnp.float32, jnp.bfloat16
    hbm = pl.BlockSpec(memory_space=pl.ANY)
    vmem = pl.BlockSpec(memory_space=pltpu.VMEM)
    dma = pltpu.SemaphoreType.DMA
    total = pl.pallas_call(
        functools.partial(kernel, sites, sectors, width, phys, depth),
        out_shape=pltpu.VMEM((rows, width), f32),
        in_specs=[hbm] * 5,
        out_specs=vmem,
        scratch_shapes=[
            pltpu.VMEM((width * phys, inner), bf16),
            pltpu.VMEM((width * depth, inner), bf16),
            pltpu.VMEM((depth, phys), bf16),
            pltpu.SMEM((1, depth), jnp.int32),
            pltpu.VMEM((rows, width), bf16),
            pltpu.VMEM((depth, width, inner), f32),
            pltpu.VMEM((depth, width, inner), bf16),
            pltpu.VMEM((width, 3 * inner), bf16),
            pltpu.VMEM((width, 3 * inner), bf16),
        ]
        + [pltpu.VMEM((rows, width), f32)] * 5
        + [dma((SLABS,)), dma((4,))]
        + [dma((chunks,))] * 6,
        compiler_params=pltpu.CompilerParams(collective_id=0, has_side_effects=True),
    )(
        boundary.reshape(width * phys, inner),
        peps_row[0].T,
        sketch.reshape(width * depth, inner),
        charges,
        left_edge,
    )
    return total[None]


def solution(mesh):
    in_specs = (
        P("site", "sector", None, None),
        P("site", None, None),
        P("site", "sector", None, None),
        P("site", None),
        P(None, "sector"),
    )
    out_specs = P("site", None, "sector")
    body = functools.partial(local, mesh.shape["site"], mesh.shape["sector"])
    return jax.shard_map(body, mesh=mesh, in_specs=in_specs, out_specs=out_specs, check_vma=False)
```

```python
import functools

import jax
import jax.numpy as jnp
from jax import lax
from jax.experimental import pallas as pl
from jax.experimental.pallas import tpu as pltpu
from jax.sharding import PartitionSpec as P

MESH = pl.DeviceIdType.MESH
CHUNK_ROWS = 32
LAG = 3
LAG_FIRST = 4
SLABS = (4, 4)
BUILDS = (4, 8)
EIGHTHS = 8


def dot(a, b):
    return jnp.dot(a, b, preferred_element_type=jnp.float32)


def split(x):
    high = x.astype(jnp.bfloat16)
    low = (x - high.astype(jnp.float32)).astype(jnp.bfloat16)
    return high, low


def iota(shape, axis):
    return lax.broadcasted_iota(jnp.int32, shape, axis)


def kernel(
    sites,
    sectors,
    width,
    phys,
    depth,
    boundary_ref,
    peps_ref,
    sketch_ref,
    charges_ref,
    left_ref,
    total,
    boundary,
    sketch,
    peps,
    charges,
    left,
    absorbed,
    sorted_sketch,
    map_high,
    map_low,
    state,
    from_below,
    from_above,
    upward,
    downward,
    boundary_sem,
    small_sem,
    state_send,
    state_recv,
    up_send,
    up_recv,
    down_send,
    down_recv,
):
    site = lax.axis_index("site")
    sector = lax.axis_index("sector")
    rows = left_ref.shape[0]
    chunks = rows // CHUNK_ROWS
    f32, bf16 = jnp.float32, jnp.bfloat16

    peps_copy = pltpu.make_async_copy(peps_ref, peps, small_sem.at[0])
    charges_copy = pltpu.make_async_copy(charges_ref, charges, small_sem.at[1])
    sketch_copy = pltpu.make_async_copy(sketch_ref, sketch, small_sem.at[2])
    left_copy = pltpu.make_async_copy(left_ref, left, small_sem.at[3])
    peps_copy.start()
    charges_copy.start()
    sketch_copy.start()
    unit = width // EIGHTHS
    slabs, edges = [], [0]
    for i, units in enumerate(SLABS):
        edges.append(edges[-1] + units * unit)
        part = pl.ds(edges[i] * phys, units * unit * phys)
        copy = pltpu.make_async_copy(boundary_ref.at[part], boundary.at[part], boundary_sem.at[i])
        copy.start()
        slabs.append(copy)

    @pl.when(site == 0)
    def _():
        left_copy.start()

    barrier = pltpu.get_barrier_semaphore()
    has_prev, has_next = site > 0, site < sites - 1
    has_below, has_above = sector > 0, sector < sectors - 1

    def greet(condition, target):
        @pl.when(condition)
        def _():
            pl.semaphore_signal(barrier, inc=1, device_id=target, device_id_type=MESH)

    prev_id, next_id = (site - 1, sector), (site + 1, sector)
    below_id, above_id = (site, sector - 1), (site, sector + 1)
    greet(has_prev, prev_id)
    greet(has_next, next_id)
    greet(has_below, below_id)
    greet(has_above, above_id)

    @pl.when(jnp.logical_not(has_below))
    def _():
        from_below[...] = jnp.zeros_like(from_below)

    @pl.when(jnp.logical_not(has_above))
    def _():
        from_above[...] = jnp.zeros_like(from_above)

    group = width // phys
    size = group * depth
    run = width // depth
    order = (
        iota((width, width), 1) == (iota((width, width), 0) % run) * depth + iota((width, width), 0) // run
    ).astype(f32).astype(bf16)
    pick = (iota((size, depth), 0) // group == iota((size, depth), 1)).astype(f32).astype(bf16)
    tile = (iota((phys, width), 1) % phys == iota((phys, width), 0)).astype(f32).astype(bf16)
    same = iota((size, width), 0) % group == iota((size, width), 1) // phys
    peps_copy.wait()
    charges_copy.wait()
    by_row = dot(pick, peps[...]).astype(bf16)
    spread = jnp.where(same, dot(by_row, tile), 0.0).astype(bf16)
    flags = [
        [(charges[0, l] == s - 1).astype(f32) for l in range(depth)] for s in range(3)
    ]

    sketch_copy.wait()
    for g in range(depth):
        moved = dot(order, sketch[pl.ds(g * width, width), :]).astype(bf16)
        for l in range(depth):
            sorted_sketch[l, pl.ds(g * run, run), :] = moved[l * run : (l + 1) * run]

    def absorb(g):
        grown = dot(spread, boundary[pl.ds(g * group * phys, width), :])
        for l in range(depth):
            absorbed[l, pl.ds(g * group, group), :] = grown[l * group : (l + 1) * group]

    def build(start, stop):
        part = pl.ds(start, stop - start)
        sums = [None] * 3
        for l in range(depth):
            high, low = split(absorbed[l, part])
            both = dot(jnp.concatenate([high, low], axis=0), sorted_sketch[l])
            product = both[: stop - start] + both[stop - start :]
            for s in range(3):
                term = flags[s][l] * product
                sums[s] = term if sums[s] is None else sums[s] + term
        for s in range(3):
            high, low = split(sums[s])
            map_high[part, pl.ds(s * width, width)] = high
            map_low[part, pl.ds(s * width, width)] = low

    built = 0
    for i, slab in enumerate(slabs):
        slab.wait()
        for g in range(edges[i] // group, edges[i + 1] // group):
            absorb(g)
        if BUILDS[i] * unit > built:
            build(built, BUILDS[i] * unit)
            built = BUILDS[i] * unit

    @pl.when(site == 0)
    def _():
        left_copy.wait()
        state[...] = left[...].astype(f32)

    degree = (
        has_prev.astype(jnp.int32)
        + has_next.astype(jnp.int32)
        + has_below.astype(jnp.int32)
        + has_above.astype(jnp.int32)
    )
    pl.semaphore_wait(barrier, degree)

    def at(ref, k):
        return ref.at[pl.ds(k * CHUNK_ROWS, CHUNK_ROWS)]

    def state_copy(k):
        return pltpu.make_async_remote_copy(
            src_ref=at(total, k), dst_ref=at(state, k), send_sem=state_send.at[k],
            recv_sem=state_recv.at[k], device_id=next_id, device_id_type=MESH,
        )

    def up_copy(k):
        return pltpu.make_async_remote_copy(
            src_ref=at(upward, k), dst_ref=at(from_below, k), send_sem=up_send.at[k],
            recv_sem=up_recv.at[k], device_id=above_id, device_id_type=MESH,
        )

    def down_copy(k):
        return pltpu.make_async_remote_copy(
            src_ref=at(downward, k), dst_ref=at(from_above, k), send_sem=down_send.at[k],
            recv_sem=down_recv.at[k], device_id=below_id, device_id_type=MESH,
        )

    def advance(k):
        @pl.when(has_prev)
        def _():
            state_copy(k).wait_recv()

        high, low = split(at(state, k)[...])
        both = jnp.concatenate([high, low], axis=0)

        def part(s):
            columns = pl.ds(s * width, width)
            twice = dot(both, map_high[:, columns])
            return twice[:CHUNK_ROWS] + (twice[CHUNK_ROWS:] + dot(high, map_low[:, columns]))

        at(upward, k)[...] = part(2)
        at(downward, k)[...] = part(0)
        at(total, k)[...] = part(1)

        @pl.when(has_above)
        def _():
            up_copy(k).start()

        @pl.when(has_below)
        def _():
            down_copy(k).start()

    def finish(k):
        @pl.when(has_below)
        def _():
            up_copy(k).wait_recv()

        @pl.when(has_above)
        def _():
            down_copy(k).wait_recv()

        at(total, k)[...] += at(from_below, k)[...] + at(from_above, k)[...]

        @pl.when(has_next)
        def _():
            state_copy(k).start()

    def stream(lag):
        for k in range(chunks + lag):
            if k < chunks:
                advance(k)
            if k >= lag:
                finish(k - lag)

    @pl.when(site == 0)
    def _():
        stream(LAG_FIRST)

    @pl.when(site > 0)
    def _():
        stream(LAG)

    for k in range(chunks):
        @pl.when(has_above)
        def _():
            up_copy(k).wait_send()

        @pl.when(has_below)
        def _():
            down_copy(k).wait_send()

        @pl.when(has_next)
        def _():
            state_copy(k).wait_send()


def store(total, out_ref, sem):
    copy = pltpu.make_async_copy(total, out_ref, sem)
    copy.start()
    copy.wait()


def local(sites, sectors, boundary, peps_row, sketch, charges, left_edge):
    _, width, phys, inner = boundary.shape
    depth = peps_row.shape[2]
    rows = left_edge.shape[0]
    chunks = rows // CHUNK_ROWS
    f32, bf16 = jnp.float32, jnp.bfloat16
    hbm = pl.BlockSpec(memory_space=pl.ANY)
    vmem = pl.BlockSpec(memory_space=pltpu.VMEM)
    dma = pltpu.SemaphoreType.DMA
    total = pl.pallas_call(
        functools.partial(kernel, sites, sectors, width, phys, depth),
        out_shape=pltpu.VMEM((rows, width), f32),
        in_specs=[hbm] * 5,
        out_specs=vmem,
        scratch_shapes=[
            pltpu.VMEM((width * phys, inner), bf16),
            pltpu.VMEM((width * depth, inner), bf16),
            pltpu.VMEM((depth, phys), bf16),
            pltpu.SMEM((1, depth), jnp.int32),
            pltpu.VMEM((rows, width), bf16),
            pltpu.VMEM((depth, width, inner), f32),
            pltpu.VMEM((depth, width, inner), bf16),
            pltpu.VMEM((width, 3 * inner), bf16),
            pltpu.VMEM((width, 3 * inner), bf16),
        ]
        + [pltpu.VMEM((rows, width), f32)] * 5
        + [dma((len(SLABS),)), dma((4,))]
        + [dma((chunks,))] * 6,
        compiler_params=pltpu.CompilerParams(collective_id=0, has_side_effects=True),
    )(
        boundary.reshape(width * phys, inner),
        peps_row[0].T,
        sketch.reshape(width * depth, inner),
        charges,
        left_edge,
    )
    return total[None]


def solution(mesh):
    in_specs = (
        P("site", "sector", None, None),
        P("site", None, None),
        P("site", "sector", None, None),
        P("site", None),
        P(None, "sector"),
    )
    out_specs = P("site", None, "sector")
    body = functools.partial(local, mesh.shape["site"], mesh.shape["sector"])
    return jax.shard_map(body, mesh=mesh, in_specs=in_specs, out_specs=out_specs, check_vma=False)
```

```python
import functools

import jax
import jax.numpy as jnp
from jax import lax
from jax.experimental import pallas as pl
from jax.experimental.pallas import tpu as pltpu
from jax.sharding import PartitionSpec as P

MESH = pl.DeviceIdType.MESH
CHUNK_ROWS = 32
LAG = 3
LAG_FIRST = 4
SLABS = (4, 4)
BUILDS = (4, 8)
EIGHTHS = 8


def dot(a, b):
    return jnp.dot(a, b, preferred_element_type=jnp.float32)


def split(x):
    high = x.astype(jnp.bfloat16)
    low = (x - high.astype(jnp.float32)).astype(jnp.bfloat16)
    return high, low


def iota(shape, axis):
    return lax.broadcasted_iota(jnp.int32, shape, axis)


def kernel(
    sites,
    sectors,
    width,
    phys,
    depth,
    boundary_ref,
    peps_ref,
    sketch_ref,
    charges_ref,
    left_ref,
    total,
    boundary,
    sketch,
    peps,
    charges,
    left,
    absorbed,
    sorted_sketch,
    map_high,
    map_low,
    state,
    from_far,
    from_near,
    to_far,
    to_near,
    boundary_sem,
    small_sem,
    state_send,
    state_recv,
    far_send,
    far_recv,
    near_send,
    near_recv,
):
    site = lax.axis_index("site")
    sector = lax.axis_index("sector")
    rows = left_ref.shape[0]
    f32, bf16 = jnp.float32, jnp.bfloat16

    peps_copy = pltpu.make_async_copy(peps_ref, peps, small_sem.at[0])
    charges_copy = pltpu.make_async_copy(charges_ref, charges, small_sem.at[1])
    sketch_copy = pltpu.make_async_copy(sketch_ref, sketch, small_sem.at[2])
    left_copy = pltpu.make_async_copy(left_ref, left, small_sem.at[3])
    peps_copy.start()
    charges_copy.start()
    sketch_copy.start()
    unit = width // EIGHTHS
    slabs, edges = [], [0]
    for i, units in enumerate(SLABS):
        edges.append(edges[-1] + units * unit)
        part = pl.ds(edges[i] * phys, units * unit * phys)
        copy = pltpu.make_async_copy(boundary_ref.at[part], boundary.at[part], boundary_sem.at[i])
        copy.start()
        slabs.append(copy)

    @pl.when(site == 0)
    def _():
        left_copy.start()

    barrier = pltpu.get_barrier_semaphore()
    step = 2 * (sector % 2) - 1
    far, near = sector + step, sector - step
    has_prev, has_next = site > 0, site < sites - 1
    has_far = jnp.logical_and(far >= 0, far < sectors)
    has_near = jnp.logical_and(near >= 0, near < sectors)

    def greet(condition, target):
        @pl.when(condition)
        def _():
            pl.semaphore_signal(barrier, inc=1, device_id=target, device_id_type=MESH)

    prev_id, next_id = (site - 1, sector), (site + 1, sector)
    far_id, near_id = (site, far), (site, near)
    greet(has_prev, prev_id)
    greet(has_next, next_id)
    greet(has_far, far_id)
    greet(has_near, near_id)

    @pl.when(jnp.logical_not(has_far))
    def _():
        from_far[...] = jnp.zeros_like(from_far)

    @pl.when(jnp.logical_not(has_near))
    def _():
        from_near[...] = jnp.zeros_like(from_near)

    group = width // phys
    size = group * depth
    run = width // depth
    def quotient(values, divisor, limit):
        return sum((values >= divisor * j).astype(jnp.int32) for j in range(1, limit))

    position = iota((width, 1), 0)
    slot = quotient(position, run, depth)
    order = (iota((width, width), 1) == (position - slot * run) * depth + slot).astype(f32).astype(bf16)
    level = quotient(iota((size, 1), 0), group, depth)
    member = iota((size, 1), 0) - level * group
    pick = (level == iota((size, depth), 1)).astype(f32).astype(bf16)
    owner = quotient(iota((1, width), 1), phys, group)
    tile = (iota((1, width), 1) - owner * phys == iota((phys, width), 0)).astype(f32).astype(bf16)
    same = member == owner
    peps_copy.wait()
    charges_copy.wait()
    by_row = dot(pick, peps[...]).astype(bf16)
    spread = jnp.where(same, dot(by_row, tile), 0.0).astype(bf16)
    flags = [
        [(charges[0, l] == s - 1).astype(f32) for l in range(depth)] for s in range(3)
    ]

    sketch_copy.wait()
    for g in range(depth):
        moved = dot(order, sketch[pl.ds(g * width, width), :]).astype(bf16)
        for l in range(depth):
            sorted_sketch[l, pl.ds(g * run, run), :] = moved[l * run : (l + 1) * run]

    def absorb(g):
        grown = dot(spread, boundary[pl.ds(g * group * phys, width), :])
        for l in range(depth):
            absorbed[l, pl.ds(g * group, group), :] = grown[l * group : (l + 1) * group]

    def build(start, stop):
        part = pl.ds(start, stop - start)
        sums = [None] * 3
        for l in range(depth):
            high, low = split(absorbed[l, part])
            both = dot(jnp.concatenate([high, low], axis=0), sorted_sketch[l])
            product = both[: stop - start] + both[stop - start :]
            for s in range(3):
                term = flags[s][l] * product
                sums[s] = term if sums[s] is None else sums[s] + term
        for s in range(3):
            high, low = split(sums[s])
            map_high[part, pl.ds(s * width, width)] = high
            map_low[part, pl.ds(s * width, width)] = low

    built = 0
    for i, slab in enumerate(slabs):
        slab.wait()
        for g in range(edges[i] // group, edges[i + 1] // group):
            absorb(g)
        if BUILDS[i] * unit > built:
            build(built, BUILDS[i] * unit)
            built = BUILDS[i] * unit

    @pl.when(site == 0)
    def _():
        left_copy.wait()

    degree = (
        has_prev.astype(jnp.int32)
        + has_next.astype(jnp.int32)
        + has_far.astype(jnp.int32)
        + has_near.astype(jnp.int32)
    )
    pl.semaphore_wait(barrier, degree)

    chunks = rows // CHUNK_ROWS
    far_columns = pl.ds(pl.multiple_of((step + 1) * width, width), width)
    near_columns = pl.ds(pl.multiple_of((1 - step) * width, width), width)
    centre_columns = pl.ds(width, width)

    def at(ref, k):
        return ref.at[pl.ds(k * CHUNK_ROWS, CHUNK_ROWS)]

    def remote(source, target, send_sem, recv_sem, k, device):
        return pltpu.make_async_remote_copy(
            src_ref=at(source, k), dst_ref=at(target, k), send_sem=send_sem.at[k],
            recv_sem=recv_sem.at[k], device_id=device, device_id_type=MESH,
        )

    def state_copy(k):
        return remote(total, state, state_send, state_recv, k, next_id)

    def far_copy(k):
        return remote(to_far, from_far, far_send, far_recv, k, far_id)

    def near_copy(k):
        return remote(to_near, from_near, near_send, near_recv, k, near_id)

    def advance(k, first):
        @pl.when(has_prev)
        def _():
            state_copy(k).wait_recv()

        if first:
            high = at(left, k)[...]
        else:
            high, low = split(at(state, k)[...])
            both = jnp.concatenate([high, low], axis=0)

        def part(columns):
            if first:
                return dot(high, map_high[:, columns]) + dot(high, map_low[:, columns])
            twice = dot(both, map_high[:, columns])
            return twice[:CHUNK_ROWS] + (twice[CHUNK_ROWS:] + dot(high, map_low[:, columns]))

        def send_far():
            @pl.when(has_far)
            def _():
                far_copy(k).start()

        def send_near():
            @pl.when(has_near)
            def _():
                near_copy(k).start()

        at(to_far, k)[...] = part(far_columns)
        if not first:
            send_far()
        at(to_near, k)[...] = part(near_columns)
        at(total, k)[...] = part(centre_columns)
        if first:
            send_far()
        send_near()

    def finish(k, first):
        @pl.when(has_near)
        def _():
            near_copy(k).wait_recv()

        @pl.when(has_far)
        def _():
            far_copy(k).wait_recv()

        at(total, k)[...] += at(from_near, k)[...] + at(from_far, k)[...]

        @pl.when(has_next)
        def _():
            state_copy(k).start()

    def stream(lag, first):
        for k in range(chunks + lag):
            if k < chunks:
                advance(k, first)
            if k >= lag:
                finish(k - lag, first)

    @pl.when(site == 0)
    def _():
        stream(LAG_FIRST, True)

    @pl.when(site > 0)
    def _():
        stream(LAG, False)

    for k in range(chunks):
        @pl.when(has_far)
        def _():
            far_copy(k).wait_send()

        @pl.when(has_near)
        def _():
            near_copy(k).wait_send()

        @pl.when(has_next)
        def _():
            state_copy(k).wait_send()


def local(sites, sectors, boundary, peps_row, sketch, charges, left_edge):
    _, width, phys, inner = boundary.shape
    depth = peps_row.shape[2]
    rows = left_edge.shape[0]
    chunks = rows // CHUNK_ROWS
    f32, bf16 = jnp.float32, jnp.bfloat16
    hbm = pl.BlockSpec(memory_space=pl.ANY)
    vmem = pl.BlockSpec(memory_space=pltpu.VMEM)
    dma = pltpu.SemaphoreType.DMA
    total = pl.pallas_call(
        functools.partial(kernel, sites, sectors, width, phys, depth),
        out_shape=pltpu.VMEM((rows, width), f32),
        in_specs=[hbm] * 5,
        out_specs=vmem,
        scratch_shapes=[
            pltpu.VMEM((width * phys, inner), bf16),
            pltpu.VMEM((width * depth, inner), bf16),
            pltpu.VMEM((depth, phys), bf16),
            pltpu.SMEM((1, depth), jnp.int32),
            pltpu.VMEM((rows, width), bf16),
            pltpu.VMEM((depth, width, inner), f32),
            pltpu.VMEM((depth, width, inner), bf16),
            pltpu.VMEM((width, 3 * inner), bf16),
            pltpu.VMEM((width, 3 * inner), bf16),
        ]
        + [pltpu.VMEM((rows, width), f32)] * 5
        + [dma((len(SLABS),)), dma((4,))]
        + [dma((chunks,))] * 6,
        compiler_params=pltpu.CompilerParams(collective_id=0, has_side_effects=True),
    )(
        boundary.reshape(width * phys, inner),
        peps_row[0].T,
        sketch.reshape(width * depth, inner),
        charges,
        left_edge,
    )
    return total[None]


def solution(mesh):
    in_specs = (
        P("site", "sector", None, None),
        P("site", None, None),
        P("site", "sector", None, None),
        P("site", None),
        P(None, "sector"),
    )
    out_specs = P("site", None, "sector")
    body = functools.partial(local, mesh.shape["site"], mesh.shape["sector"])
    return jax.shard_map(body, mesh=mesh, in_specs=in_specs, out_specs=out_specs, check_vma=False)
```

```python
import functools

import jax
import jax.numpy as jnp
from jax import lax
from jax.experimental import pallas as pl
from jax.experimental.pallas import tpu as pltpu
from jax.sharding import PartitionSpec as P

MESH = pl.DeviceIdType.MESH
CHUNK_ROWS = 32
LAG = 3
LAG_FIRST = 4
SLABS = (4, 4)
BUILDS = (4, 8)
EIGHTHS = 8


def dot(a, b):
    return jnp.dot(a, b, preferred_element_type=jnp.float32)


def split(x):
    high = x.astype(jnp.bfloat16)
    low = (x - high.astype(jnp.float32)).astype(jnp.bfloat16)
    return high, low


def iota(shape, axis):
    return lax.broadcasted_iota(jnp.int32, shape, axis)


def kernel(
    sites,
    sectors,
    width,
    phys,
    depth,
    boundary_ref,
    peps_ref,
    sketch_ref,
    charges_ref,
    left_ref,
    total,
    boundary,
    sketch,
    peps,
    charges,
    left,
    absorbed,
    sorted_sketch,
    map_high,
    map_low,
    state,
    from_far,
    from_near,
    to_far,
    to_near,
    boundary_sem,
    small_sem,
):
    site = lax.axis_index("site")
    sector = lax.axis_index("sector")
    rows = left_ref.shape[0]
    f32, bf16 = jnp.float32, jnp.bfloat16

    peps_copy = pltpu.make_async_copy(peps_ref, peps, small_sem.at[0])
    charges_copy = pltpu.make_async_copy(charges_ref, charges, small_sem.at[1])
    sketch_copy = pltpu.make_async_copy(sketch_ref, sketch, small_sem.at[2])
    left_copy = pltpu.make_async_copy(left_ref, left, small_sem.at[3])
    peps_copy.start()
    charges_copy.start()
    sketch_copy.start()
    unit = width // EIGHTHS
    slabs, edges = [], [0]
    for i, units in enumerate(SLABS):
        edges.append(edges[-1] + units * unit)
        part = pl.ds(edges[i] * phys, units * unit * phys)
        copy = pltpu.make_async_copy(boundary_ref.at[part], boundary.at[part], boundary_sem.at[i])
        copy.start()
        slabs.append(copy)

    @pl.when(site == 0)
    def _():
        left_copy.start()

    def scoped(state_send, state_recv, far_send, far_recv, near_send, near_recv):
        barrier = pltpu.get_barrier_semaphore()
        step = 2 * (sector % 2) - 1
        far, near = sector + step, sector - step
        has_prev, has_next = site > 0, site < sites - 1
        has_far = jnp.logical_and(far >= 0, far < sectors)
        has_near = jnp.logical_and(near >= 0, near < sectors)

        def greet(condition, target):
            @pl.when(condition)
            def _():
                pl.semaphore_signal(barrier, inc=1, device_id=target, device_id_type=MESH)

        prev_id, next_id = (site - 1, sector), (site + 1, sector)
        far_id, near_id = (site, far), (site, near)
        greet(has_prev, prev_id)
        greet(has_next, next_id)
        greet(has_far, far_id)
        greet(has_near, near_id)

        @pl.when(jnp.logical_not(has_far))
        def _():
            from_far[...] = jnp.zeros_like(from_far)

        @pl.when(jnp.logical_not(has_near))
        def _():
            from_near[...] = jnp.zeros_like(from_near)

        group = width // phys
        size = group * depth
        run = width // depth
        def quotient(values, divisor, limit):
            return sum((values >= divisor * j).astype(jnp.int32) for j in range(1, limit))

        position = iota((width, 1), 0)
        slot = quotient(position, run, depth)
        order = (iota((width, width), 1) == (position - slot * run) * depth + slot).astype(f32).astype(bf16)
        level = quotient(iota((size, 1), 0), group, depth)
        member = iota((size, 1), 0) - level * group
        pick = (level == iota((size, depth), 1)).astype(f32).astype(bf16)
        owner = quotient(iota((1, width), 1), phys, group)
        tile = (iota((1, width), 1) - owner * phys == iota((phys, width), 0)).astype(f32).astype(bf16)
        same = member == owner
        peps_copy.wait()
        charges_copy.wait()
        by_row = dot(pick, peps[...]).astype(bf16)
        spread = jnp.where(same, dot(by_row, tile), 0.0).astype(bf16)
        flags = [
            [(charges[0, l] == s - 1).astype(f32) for l in range(depth)] for s in range(3)
        ]

        sketch_copy.wait()
        for g in range(depth):
            moved = dot(order, sketch[pl.ds(g * width, width), :]).astype(bf16)
            for l in range(depth):
                sorted_sketch[l, pl.ds(g * run, run), :] = moved[l * run : (l + 1) * run]

        def absorb(g):
            grown = dot(spread, boundary[pl.ds(g * group * phys, width), :])
            for l in range(depth):
                absorbed[l, pl.ds(g * group, group), :] = grown[l * group : (l + 1) * group]

        def build(start, stop):
            part = pl.ds(start, stop - start)
            sums = [None] * 3
            for l in range(depth):
                high, low = split(absorbed[l, part])
                both = dot(jnp.concatenate([high, low], axis=0), sorted_sketch[l])
                product = both[: stop - start] + both[stop - start :]
                for s in range(3):
                    term = flags[s][l] * product
                    sums[s] = term if sums[s] is None else sums[s] + term
            for s in range(3):
                high, low = split(sums[s])
                map_high[part, pl.ds(s * width, width)] = high
                map_low[part, pl.ds(s * width, width)] = low

        built = 0
        for i, slab in enumerate(slabs):
            slab.wait()
            for g in range(edges[i] // group, edges[i + 1] // group):
                absorb(g)
            if BUILDS[i] * unit > built:
                build(built, BUILDS[i] * unit)
                built = BUILDS[i] * unit

        @pl.when(site == 0)
        def _():
            left_copy.wait()

        degree = (
            has_prev.astype(jnp.int32)
            + has_next.astype(jnp.int32)
            + has_far.astype(jnp.int32)
            + has_near.astype(jnp.int32)
        )
        pl.semaphore_wait(barrier, degree)

        chunks = rows // CHUNK_ROWS
        far_columns = pl.ds(pl.multiple_of((step + 1) * width, width), width)
        near_columns = pl.ds(pl.multiple_of((1 - step) * width, width), width)
        centre_columns = pl.ds(width, width)

        def at(ref, k):
            return ref.at[pl.ds(k * CHUNK_ROWS, CHUNK_ROWS)]

        def remote(source, target, send_sem, recv_sem, k, device):
            return pltpu.make_async_remote_copy(
                src_ref=at(source, k), dst_ref=at(target, k), send_sem=send_sem,
                recv_sem=recv_sem.at[k], device_id=device, device_id_type=MESH,
            )

        def state_copy(k):
            return remote(total, state, state_send, state_recv, k, next_id)

        def far_copy(k):
            return remote(to_far, from_far, far_send, far_recv, k, far_id)

        def near_copy(k):
            return remote(to_near, from_near, near_send, near_recv, k, near_id)

        def advance(k, first):
            @pl.when(has_prev)
            def _():
                state_copy(k).wait_recv()

            if first:
                high = at(left, k)[...]
            else:
                high, low = split(at(state, k)[...])
                both = jnp.concatenate([high, low], axis=0)

            def part(columns):
                if first:
                    return dot(high, map_high[:, columns]) + dot(high, map_low[:, columns])
                twice = dot(both, map_high[:, columns])
                return twice[:CHUNK_ROWS] + (twice[CHUNK_ROWS:] + dot(high, map_low[:, columns]))

            def send_far():
                @pl.when(has_far)
                def _():
                    far_copy(k).start()

            def send_near():
                @pl.when(has_near)
                def _():
                    near_copy(k).start()

            at(to_far, k)[...] = part(far_columns)
            if not first:
                send_far()
            at(to_near, k)[...] = part(near_columns)
            at(total, k)[...] = part(centre_columns)
            if first:
                send_far()
            send_near()

        def finish(k, first):
            @pl.when(has_near)
            def _():
                near_copy(k).wait_recv()

            @pl.when(has_far)
            def _():
                far_copy(k).wait_recv()

            at(total, k)[...] += at(from_near, k)[...] + at(from_far, k)[...]

            @pl.when(has_next)
            def _():
                state_copy(k).start()

        def stream(lag, first):
            for k in range(chunks + lag):
                if k < chunks:
                    advance(k, first)
                if k >= lag:
                    finish(k - lag, first)

        @pl.when(site == 0)
        def _():
            stream(LAG_FIRST, True)

        @pl.when(site > 0)
        def _():
            stream(LAG, False)

        def sent(source, target, send_sem, recv_sem, device):
            pltpu.make_async_remote_copy(
                src_ref=source, dst_ref=target, send_sem=send_sem, recv_sem=recv_sem.at[0],
                device_id=device, device_id_type=MESH,
            ).wait_send()

        @pl.when(has_near)
        def _():
            sent(to_near, from_near, near_send, near_recv, near_id)

        @pl.when(has_far)
        def _():
            sent(to_far, from_far, far_send, far_recv, far_id)

        @pl.when(has_next)
        def _():
            sent(total, state, state_send, state_recv, next_id)

    dma = pltpu.SemaphoreType.DMA
    pl.run_scoped(scoped, *[dma(()), dma((rows // CHUNK_ROWS,))] * 3)


def local(sites, sectors, boundary, peps_row, sketch, charges, left_edge):
    _, width, phys, inner = boundary.shape
    depth = peps_row.shape[2]
    rows = left_edge.shape[0]
    f32, bf16 = jnp.float32, jnp.bfloat16
    hbm = pl.BlockSpec(memory_space=pl.ANY)
    vmem = pl.BlockSpec(memory_space=pltpu.VMEM)
    dma = pltpu.SemaphoreType.DMA
    total = pl.pallas_call(
        functools.partial(kernel, sites, sectors, width, phys, depth),
        out_shape=pltpu.VMEM((rows, width), f32),
        in_specs=[hbm] * 5,
        out_specs=vmem,
        scratch_shapes=[
            pltpu.VMEM((width * phys, inner), bf16),
            pltpu.VMEM((width * depth, inner), bf16),
            pltpu.VMEM((depth, phys), bf16),
            pltpu.SMEM((1, depth), jnp.int32),
            pltpu.VMEM((rows, width), bf16),
            pltpu.VMEM((depth, width, inner), f32),
            pltpu.VMEM((depth, width, inner), bf16),
            pltpu.VMEM((width, 3 * inner), bf16),
            pltpu.VMEM((width, 3 * inner), bf16),
        ]
        + [pltpu.VMEM((rows, width), f32)] * 5
        + [dma((len(SLABS),)), dma((4,))],
        compiler_params=pltpu.CompilerParams(collective_id=0, has_side_effects=True),
    )(
        boundary.reshape(width * phys, inner),
        peps_row[0].T,
        sketch.reshape(width * depth, inner),
        charges,
        left_edge,
    )
    return total[None]


def solution(mesh):
    in_specs = (
        P("site", "sector", None, None),
        P("site", None, None),
        P("site", "sector", None, None),
        P("site", None),
        P(None, "sector"),
    )
    out_specs = P("site", None, "sector")
    body = functools.partial(local, mesh.shape["site"], mesh.shape["sector"])
    return jax.shard_map(body, mesh=mesh, in_specs=in_specs, out_specs=out_specs, check_vma=False)
```

```python
import functools

import jax
import jax.numpy as jnp
from jax import lax
from jax.experimental import pallas as pl
from jax.experimental.pallas import tpu as pltpu
from jax.sharding import PartitionSpec as P

MESH = pl.DeviceIdType.MESH
CHUNK_ROWS = 32
LAG = 3
LAG_FIRST = 4
SLABS = (4, 4)
BUILDS = (4, 8)
EIGHTHS = 8


def dot(a, b):
    return jnp.dot(a, b, preferred_element_type=jnp.float32)


def split(x):
    high = x.astype(jnp.bfloat16)
    low = (x - high.astype(jnp.float32)).astype(jnp.bfloat16)
    return high, low


def iota(shape, axis):
    return lax.broadcasted_iota(jnp.int32, shape, axis)


def kernel(
    sites,
    sectors,
    width,
    phys,
    depth,
    boundary_ref,
    peps_ref,
    sketch_ref,
    charges_ref,
    left_ref,
    total,
    boundary,
    sketch,
    peps,
    charges,
    left,
    absorbed,
    sorted_sketch,
    map_high,
    map_low,
    state,
    from_far,
    from_near,
    to_far,
    to_near,
    boundary_sem,
    small_sem,
):
    site = lax.axis_index("site")
    sector = lax.axis_index("sector")
    rows = left_ref.shape[0]
    f32, bf16 = jnp.float32, jnp.bfloat16

    peps_copy = pltpu.make_async_copy(peps_ref, peps, small_sem.at[0])
    charges_copy = pltpu.make_async_copy(charges_ref, charges, small_sem.at[1])
    sketch_copy = pltpu.make_async_copy(sketch_ref, sketch, small_sem.at[2])
    left_copy = pltpu.make_async_copy(left_ref, left, small_sem.at[3])
    peps_copy.start()
    charges_copy.start()
    sketch_copy.start()
    unit = width // EIGHTHS
    slabs, edges = [], [0]
    for i, units in enumerate(SLABS):
        edges.append(edges[-1] + units * unit)
        part = pl.ds(edges[i] * phys, units * unit * phys)
        copy = pltpu.make_async_copy(boundary_ref.at[part], boundary.at[part], boundary_sem.at[i])
        copy.start()
        slabs.append(copy)

    @pl.when(site == 0)
    def _():
        left_copy.start()

    def scoped(state_send, state_recv, far_send, far_recv, near_send, near_recv):
        barrier = pltpu.get_barrier_semaphore()
        step = 2 * (sector % 2) - 1
        far, near = sector + step, sector - step
        has_prev, has_next = site > 0, site < sites - 1
        has_far = jnp.logical_and(far >= 0, far < sectors)
        has_near = jnp.logical_and(near >= 0, near < sectors)

        def greet(condition, target):
            @pl.when(condition)
            def _():
                pl.semaphore_signal(barrier, inc=1, device_id=target, device_id_type=MESH)

        prev_id, next_id = (site - 1, sector), (site + 1, sector)
        far_id, near_id = (site, far), (site, near)
        greet(has_prev, prev_id)
        greet(has_next, next_id)
        greet(has_far, far_id)
        greet(has_near, near_id)

        @pl.when(jnp.logical_not(has_far))
        def _():
            from_far[...] = jnp.zeros_like(from_far)

        @pl.when(jnp.logical_not(has_near))
        def _():
            from_near[...] = jnp.zeros_like(from_near)

        group = width // phys
        size = group * depth
        run = width // depth
        def quotient(values, divisor, limit):
            return sum((values >= divisor * j).astype(jnp.int32) for j in range(1, limit))

        position = iota((width, 1), 0)
        slot = quotient(position, run, depth)
        order = (iota((width, width), 1) == (position - slot * run) * depth + slot).astype(f32).astype(bf16)
        level = quotient(iota((size, 1), 0), group, depth)
        member = iota((size, 1), 0) - level * group
        pick = (level == iota((size, depth), 1)).astype(f32).astype(bf16)
        owner = quotient(iota((1, width), 1), phys, group)
        tile = (iota((1, width), 1) - owner * phys == iota((phys, width), 0)).astype(f32).astype(bf16)
        same = member == owner
        peps_copy.wait()
        charges_copy.wait()
        by_row = dot(pick, peps[...]).astype(bf16)
        spread = jnp.where(same, dot(by_row, tile), 0.0).astype(bf16)
        flags = [
            [(charges[0, l] == s - 1).astype(f32) for l in range(depth)] for s in range(3)
        ]

        sketch_copy.wait()
        for g in range(depth):
            moved = dot(order, sketch[pl.ds(g * width, width), :]).astype(bf16)
            for l in range(depth):
                sorted_sketch[l, pl.ds(g * run, run), :] = moved[l * run : (l + 1) * run]

        def absorb(g):
            grown = dot(spread, boundary[pl.ds(g * group * phys, width), :])
            for l in range(depth):
                absorbed[l, pl.ds(g * group, group), :] = grown[l * group : (l + 1) * group]

        def build(start, stop):
            part = pl.ds(start, stop - start)
            sums = [None] * 3
            for l in range(depth):
                high, low = split(absorbed[l, part])
                both = dot(jnp.concatenate([high, low], axis=0), sorted_sketch[l])
                product = both[: stop - start] + both[stop - start :]
                for s in range(3):
                    term = flags[s][l] * product
                    sums[s] = term if sums[s] is None else sums[s] + term
            for s in range(3):
                high, low = split(sums[s])
                map_high[part, pl.ds(s * width, width)] = high
                map_low[part, pl.ds(s * width, width)] = low

        built = 0
        for i, slab in enumerate(slabs):
            slab.wait()
            for g in range(edges[i] // group, edges[i + 1] // group):
                absorb(g)
            if BUILDS[i] * unit > built:
                build(built, BUILDS[i] * unit)
                built = BUILDS[i] * unit

        @pl.when(site == 0)
        def _():
            left_copy.wait()

        degree = (
            has_prev.astype(jnp.int32)
            + has_next.astype(jnp.int32)
            + has_far.astype(jnp.int32)
            + has_near.astype(jnp.int32)
        )
        pl.semaphore_wait(barrier, degree)

        chunks = rows // CHUNK_ROWS
        far_columns = pl.ds(pl.multiple_of((step + 1) * width, width), width)
        near_columns = pl.ds(pl.multiple_of((1 - step) * width, width), width)
        centre_columns = pl.ds(width, width)

        def at(ref, k):
            return ref.at[pl.ds(k * CHUNK_ROWS, CHUNK_ROWS)]

        def remote(source, target, send_sem, recv_sem, k, device):
            return pltpu.make_async_remote_copy(
                src_ref=at(source, k), dst_ref=at(target, k), send_sem=send_sem,
                recv_sem=recv_sem.at[k], device_id=device, device_id_type=MESH,
            )

        def state_copy(k):
            return remote(total, state, state_send, state_recv, k, next_id)

        def far_copy(k):
            return remote(to_far, from_far, far_send, far_recv, k, far_id)

        def near_copy(k):
            return remote(to_near, from_near, near_send, near_recv, k, near_id)

        def advance(k, first):
            @pl.when(has_prev)
            def _():
                state_copy(k).wait_recv()

            if first:
                high = at(left, k)[...]
            else:
                high, low = split(at(state, k)[...])
                both = jnp.concatenate([high, low], axis=0)

            def part(columns):
                if first:
                    return dot(high, map_high[:, columns]) + dot(high, map_low[:, columns])
                twice = dot(both, map_high[:, columns])
                return twice[:CHUNK_ROWS] + (twice[CHUNK_ROWS:] + dot(high, map_low[:, columns]))

            def send_far():
                @pl.when(has_far)
                def _():
                    far_copy(k).start()

            def send_near():
                @pl.when(has_near)
                def _():
                    near_copy(k).start()

            at(to_far, k)[...] = part(far_columns)
            send_far()
            at(to_near, k)[...] = part(near_columns)
            at(total, k)[...] = part(centre_columns)
            send_near()

        def finish(k, first):
            @pl.when(has_near)
            def _():
                near_copy(k).wait_recv()

            @pl.when(has_far)
            def _():
                far_copy(k).wait_recv()

            at(total, k)[...] += at(from_near, k)[...] + at(from_far, k)[...]

            @pl.when(has_next)
            def _():
                state_copy(k).start()

        def stream(lag, first):
            for k in range(chunks + lag):
                if k < chunks:
                    advance(k, first)
                if k >= lag:
                    finish(k - lag, first)

        @pl.when(site == 0)
        def _():
            stream(LAG_FIRST, True)

        @pl.when(site > 0)
        def _():
            stream(LAG, False)

        def sent(source, target, send_sem, recv_sem, device):
            pltpu.make_async_remote_copy(
                src_ref=source, dst_ref=target, send_sem=send_sem, recv_sem=recv_sem.at[0],
                device_id=device, device_id_type=MESH,
            ).wait_send()

        @pl.when(has_near)
        def _():
            sent(to_near, from_near, near_send, near_recv, near_id)

        @pl.when(has_far)
        def _():
            sent(to_far, from_far, far_send, far_recv, far_id)

        @pl.when(has_next)
        def _():
            sent(total, state, state_send, state_recv, next_id)

    dma = pltpu.SemaphoreType.DMA
    pl.run_scoped(scoped, *[dma(()), dma((rows // CHUNK_ROWS,))] * 3)


def local(sites, sectors, boundary, peps_row, sketch, charges, left_edge):
    _, width, phys, inner = boundary.shape
    depth = peps_row.shape[2]
    rows = left_edge.shape[0]
    f32, bf16 = jnp.float32, jnp.bfloat16
    hbm = pl.BlockSpec(memory_space=pl.ANY)
    vmem = pl.BlockSpec(memory_space=pltpu.VMEM)
    dma = pltpu.SemaphoreType.DMA
    total = pl.pallas_call(
        functools.partial(kernel, sites, sectors, width, phys, depth),
        out_shape=pltpu.VMEM((rows, width), f32),
        in_specs=[hbm] * 5,
        out_specs=vmem,
        scratch_shapes=[
            pltpu.VMEM((width * phys, inner), bf16),
            pltpu.VMEM((width * depth, inner), bf16),
            pltpu.VMEM((depth, phys), bf16),
            pltpu.SMEM((1, depth), jnp.int32),
            pltpu.VMEM((rows, width), bf16),
            pltpu.VMEM((depth, width, inner), f32),
            pltpu.VMEM((depth, width, inner), bf16),
            pltpu.VMEM((width, 3 * inner), bf16),
            pltpu.VMEM((width, 3 * inner), bf16),
        ]
        + [pltpu.VMEM((rows, width), f32)] * 5
        + [dma((len(SLABS),)), dma((4,))],
        compiler_params=pltpu.CompilerParams(collective_id=0, has_side_effects=True),
    )(
        boundary.reshape(width * phys, inner),
        peps_row[0].T,
        sketch.reshape(width * depth, inner),
        charges,
        left_edge,
    )
    return total[None]


def solution(mesh):
    in_specs = (
        P("site", "sector", None, None),
        P("site", None, None),
        P("site", "sector", None, None),
        P("site", None),
        P(None, "sector"),
    )
    out_specs = P("site", None, "sector")
    body = functools.partial(local, mesh.shape["site"], mesh.shape["sector"])
    return jax.shard_map(body, mesh=mesh, in_specs=in_specs, out_specs=out_specs, check_vma=False)
```
